32 devices in a mesh: groups: 2 (over x), feat: 4 (over y, core), sub: 4 (over z).
Axes of the slice: x: 2, y: 2, z: 4, core: 2. Of those that a mesh axis runs over, the one named last changes fastest.
Arguments:
- hidden: bfloat16 [32, 8192], P('groups', 'feat'), parts along dimension 0, may hold values from -400 to 400
- input_norm_gain: bfloat16 [8192], P('feat'), may hold values from 0.25 to 1.75
- query_weight: bfloat16 [8192, 4096], P('feat', 'sub'), may hold values from -1 to 1
- key_weight: bfloat16 [8192, 512], P('feat', 'sub'), may hold values from -1 to 1
- value_weight: bfloat16 [8192, 512], P('feat', 'sub'), may hold values from -0.0625 to 0.0625
- adapter_down_weight: bfloat16 [8192, 512], P('feat'), may hold values from -0.0625 to 0.0625
- adapter_up_weight: bfloat16 [512, 4096], P(None, 'sub'), may hold values from -0.75 to 0.75
- output_weight: bfloat16 [4096, 8192], P('sub', 'feat'), may hold values from -0.09375 to 0.09375
- request_adapter: int32 [8], P('groups'), parts along dimension 0, may hold values from 0 to 7
- stored_owner: int32 [8, 4], P('groups'), parts along dimension 0, may hold values from 0 to 3, as said below
- stored_lengths: int32 [8], P('groups'), parts along dimension 0, may hold values from 2048 to 8192, as said below
- stored_keys: bfloat16 [16, 8192, 512], P(('groups', 'feat'), None, 'sub'), parts along dimension 0, may hold values from -400 to 400
- stored_values: bfloat16 [16, 8192, 512], P(('groups', 'feat'), None, 'sub'), parts along dimension 0, may hold values from -12 to 12
Outputs:
- attn_out: bfloat16 [32, 8192], P(('groups', 'sub'), 'feat'), parts along dimension 0
The draws below stay inside these ranges and needn't reach their ends.
There are 2 independent parts, one for each index of `groups`. The reference program is written for one: setup_inputs(seed, part) draws one part's arguments, and reference() takes and returns one part's arrays. A program takes and returns all parts, laid end to end along the dimension named above; an argument that names none is the same for every part. Nothing has to cross between parts.
Inputs may be any that keep to these rules, and one draw needn't show every extreme that they name: `stored_owner`: for every key-value head no owner holds more than 2 requests, and some owner holds exactly 2. `stored_lengths`: some request has exactly 8192 cached tokens and some exactly 2048.
All inputs are finite; a program needn't handle non-finite values.
Results may differ from the reference program's by a relative error of at most 0.014.
Values may be sent and summed in bfloat16 or wider, within the bound.
No kernel may reach another device: no remote copies, remote signals or barrier semaphores. Data moves between devices by JAX's collectives and lax.ppermute only.
A program may use at most 64 MiB of HBM per device.

```python
import jax
import jax.numpy as jnp
from jax import lax

MODEL_WIDTH = 8192
HEAD_SIZE = 128
GROUP = 8
ADAPTER_RANK = 64
USER_ADAPTERS = 8
REQ_DEV = 1
DRAFT = 4
CTX = 8192
KVH = 4
QUERY_HEADS = 32
REQS = 4
SLOTS = 2
TOKENS = 16
N_FEAT = 4


def draw_hidden(key, part):
    key_a = jax.random.fold_in(jax.random.fold_in(key, 11), 0)
    column = jnp.arange(MODEL_WIDTH, dtype=jnp.float32) / MODEL_WIDTH
    falling = 1.0 - column
    values = jax.random.normal(key_a, (TOKENS, MODEL_WIDTH)) * (3.0 ** falling)[None, :]
    return jnp.clip(values, -400.0, 400.0).astype(jnp.bfloat16)


def head_columns(key, head):
    head_key = jax.random.fold_in(jax.random.fold_in(key, 61), head)
    return jax.random.normal(head_key, (MODEL_WIDTH, HEAD_SIZE)) * MODEL_WIDTH ** (-0.5)


def draw_query_weight(key, part):
    blocks = jax.vmap(lambda head: head_columns(key, head))(jnp.arange(QUERY_HEADS))
    whole = jnp.transpose(blocks, (1, 0, 2)).reshape(MODEL_WIDTH, QUERY_HEADS * HEAD_SIZE)
    return jnp.clip(whole, -1.0, 1.0).astype(jnp.bfloat16)


def draw_key_weight(key, part):
    blocks = jax.vmap(lambda head: head_columns(key, head * GROUP))(jnp.arange(KVH))
    noise = jax.random.normal(jax.random.fold_in(key, 67), (KVH, MODEL_WIDTH, HEAD_SIZE)) * (0.5 * MODEL_WIDTH ** (-0.5))
    whole = jnp.transpose(blocks + noise, (1, 0, 2)).reshape(MODEL_WIDTH, KVH * HEAD_SIZE)
    return jnp.clip(whole, -1.0, 1.0).astype(jnp.bfloat16)


def owner_head(key):
    key_a, key_b, key_c = jax.random.split(key, 3)
    pool = 2 * REQS
    score = jax.random.permutation(key_a, pool).astype(jnp.int32)
    full_owner = jax.random.randint(key_b, (), 0, REQS // REQ_DEV)
    position = jnp.arange(pool)
    score = score - pool * (position // SLOTS == full_owner).astype(jnp.int32)
    chosen = jnp.argsort(score, stable=True)[:REQS]
    chosen = chosen[jax.random.permutation(key_c, REQS)]
    return (chosen // SLOTS).astype(jnp.int32)


def draw_stored_owner(key, part):
    base = jax.random.fold_in(key, 23)
    head_keys = jax.vmap(lambda index: jax.random.fold_in(base, index))(jnp.arange(KVH))
    return jax.vmap(owner_head)(head_keys).T.astype(jnp.int32)


def draw_stored_lengths(key, part):
    key_a, key_b, key_c = jax.random.split(jax.random.fold_in(key, 37), 3)
    values = jax.random.randint(key_a, (REQS,), CTX // 4, CTX + 1)
    longest = jax.random.randint(key_b, (), 0, REQS)
    shortest = (longest + 1 + jax.random.randint(key_c, (), 0, REQS - 1)) % REQS
    index = jnp.arange(REQS)
    values = jnp.where(index == longest, CTX, values)
    values = jnp.where(index == shortest, CTX // 4, values)
    return values.astype(jnp.int32)


def draw_stored_keys(key, part):
    key_a = jax.random.fold_in(jax.random.fold_in(key, 41), 0)
    row_count = N_FEAT * SLOTS
    columns = KVH * HEAD_SIZE
    array_shape = (row_count, CTX, columns)
    values = jax.random.normal(key_a, array_shape)
    return jnp.clip(values, -400.0, 400.0).astype(jnp.bfloat16)


def draw_stored_values(key, part):
    key_a, key_b = jax.random.split(jax.random.fold_in(key, 53), 2)
    array_shape = (N_FEAT * SLOTS, CTX, KVH * HEAD_SIZE)
    offset = jax.random.normal(key_b, (N_FEAT * SLOTS, 1, KVH * HEAD_SIZE))
    values = jax.random.normal(key_a, array_shape) + offset
    return jnp.clip(values, -12.0, 12.0).astype(jnp.bfloat16)


def touch_ends(drawn, rng, low, top_value):
    longest = drawn.shape.index(max(drawn.shape))
    spots = []
    for shift in (0, 1):
        where = [jax.random.randint(jax.random.fold_in(rng, axis), (), 0, length) for axis, length in enumerate(drawn.shape)]
        where[longest] = (where[longest] + shift) % drawn.shape[longest]
        spots.append(tuple(where))
    return drawn.at[spots[0]].set(low).at[spots[1]].set(top_value)


def block_levels(key, shape, cuts, low, high):
    def one(axis_at, shards_of):
        draws = jax.random.uniform(jax.random.fold_in(jax.random.fold_in(key, 6), axis_at), (shards_of,), jnp.float32, low / len(cuts), high / len(cuts))
        return jnp.repeat(jnp.exp(draws), shape[axis_at] // shards_of).reshape((-1,) + (1,) * (len(shape) - axis_at - 1))

    loudness = one(*cuts[0])
    for cut in cuts[1:]:
        loudness = loudness * one(*cut)
    return loudness


def gaussian(own_key, extent, deviation, limit, cuts=(), held_as=jnp.bfloat16):
    drawn = jax.random.normal(own_key, extent, jnp.float32) * deviation
    if len(cuts) > 0:
        drawn = block_levels(own_key, extent, cuts, -0.22, 0.18) * drawn
    return jnp.clip(drawn, min=-limit, max=limit).astype(held_as)


def setup_inputs(seed: int = 0, part: int = 0) -> dict:
    keys = jax.random.split(jax.random.key(seed), 14)
    part_keys = jax.random.split(jax.random.fold_in(keys[13], part), 14)
    hidden = draw_hidden(jax.random.fold_in(jax.random.fold_in(keys[13], part), 71), part)
    input_norm_gain = jnp.clip(1.0 + 0.15 * jax.random.normal(keys[1], (MODEL_WIDTH,), jnp.float32), 0.25, 1.75).astype(jnp.bfloat16)
    query_weight = draw_query_weight(jax.random.fold_in(keys[13], 71), part)
    key_weight = draw_key_weight(jax.random.fold_in(keys[13], 71), part)
    value_weight = gaussian(keys[4], (MODEL_WIDTH, KVH * HEAD_SIZE), MODEL_WIDTH ** -0.5, 0.0625, ((0, 4), (1, 4)))
    adapter_down_weight = gaussian(keys[5], (MODEL_WIDTH, USER_ADAPTERS * ADAPTER_RANK), MODEL_WIDTH ** -0.5, 0.0625, ((0, 4),))
    adapter_up_weight = gaussian(keys[6], (USER_ADAPTERS * ADAPTER_RANK, QUERY_HEADS * HEAD_SIZE), ADAPTER_RANK ** -0.5, 0.75, ((1, 4),))
    output_weight = gaussian(keys[7], (QUERY_HEADS * HEAD_SIZE, MODEL_WIDTH), (QUERY_HEADS * HEAD_SIZE) ** -0.5, 0.09375, ((0, 4), (1, 4)))
    request_adapter = touch_ends(jax.random.randint(part_keys[8], (REQS,), 0, USER_ADAPTERS), jax.random.fold_in(part_keys[8], 1), 0, USER_ADAPTERS - 1).astype(jnp.int32)
    stored_owner = draw_stored_owner(jax.random.fold_in(jax.random.fold_in(keys[13], part), 71), part)
    stored_lengths = draw_stored_lengths(jax.random.fold_in(jax.random.fold_in(keys[13], part), 71), part)
    stored_keys = draw_stored_keys(jax.random.fold_in(jax.random.fold_in(keys[13], part), 71), part)
    stored_values = draw_stored_values(jax.random.fold_in(jax.random.fold_in(keys[13], part), 71), part)
    return {"hidden": hidden, "input_norm_gain": input_norm_gain, "query_weight": query_weight, "key_weight": key_weight, "value_weight": value_weight, "adapter_down_weight": adapter_down_weight, "adapter_up_weight": adapter_up_weight, "output_weight": output_weight, "request_adapter": request_adapter, "stored_owner": stored_owner, "stored_lengths": stored_lengths, "stored_keys": stored_keys, "stored_values": stored_values}


norm_eps = 1e-05
rope_base = 500000.0

def rotate(values, positions):
    half_dim = values.shape[-1] // 2
    inv_freq = rope_base ** (-(jnp.arange(half_dim, dtype=jnp.float32) * 2.0) / values.shape[-1])
    angles = positions * inv_freq
    cosine = jnp.cos(angles)
    sine = jnp.sin(angles)
    first_half = values[..., :half_dim]
    second_half = values[..., half_dim:]
    return jnp.concatenate([first_half * cosine - second_half * sine, second_half * cosine + first_half * sine], axis=-1)

def slot_rows(stored_owner):
    req_iota = jnp.arange(REQS)
    earlier = req_iota[None, :] < req_iota[:, None]
    same_owner = stored_owner[None, :, :] == stored_owner[:, None, :]
    slot_index = lax.optimization_barrier(jnp.sum(jnp.logical_and(same_owner, earlier[:, :, None]).astype(jnp.int32), axis=1))
    return (stored_owner * SLOTS + slot_index).astype(jnp.int32)

def reference(hidden, input_norm_gain, query_weight, key_weight, value_weight, adapter_down_weight, adapter_up_weight, output_weight, request_adapter, stored_owner, stored_lengths, stored_keys, stored_values):
    hidden32 = hidden.astype(jnp.float32)
    mean_square = lax.optimization_barrier(jnp.mean(hidden32 * hidden32, axis=1, keepdims=True))
    normalized_hidden = (hidden32 * lax.rsqrt(mean_square + norm_eps) * input_norm_gain.astype(jnp.float32)).astype(jnp.bfloat16)
    query_unrotated = jnp.dot(normalized_hidden, query_weight, preferred_element_type=jnp.float32)
    key_pre = jnp.dot(normalized_hidden, key_weight, preferred_element_type=jnp.float32)
    value_pre = jnp.dot(normalized_hidden, value_weight, preferred_element_type=jnp.float32)
    tok_adapter = jnp.repeat(request_adapter, DRAFT)
    column_adapter = jnp.arange(USER_ADAPTERS * ADAPTER_RANK) // ADAPTER_RANK
    retain_mask = column_adapter[None, :] == tok_adapter[:, None]
    adapter_middle = jnp.where(retain_mask, jnp.dot(normalized_hidden, adapter_down_weight, preferred_element_type=jnp.float32), 0.0)
    query_unrotated = query_unrotated + jnp.dot(adapter_middle, adapter_up_weight.astype(jnp.float32), precision=lax.Precision.HIGHEST)
    positions = (jnp.repeat(stored_lengths, DRAFT) + jnp.tile(jnp.arange(DRAFT), REQS)).astype(jnp.float32)
    query = rotate(query_unrotated.reshape(TOKENS, QUERY_HEADS, HEAD_SIZE), positions[:, None, None]).astype(jnp.bfloat16)
    key_new = rotate(key_pre.reshape(TOKENS, KVH, HEAD_SIZE), positions[:, None, None]).astype(jnp.bfloat16)
    value_new = value_pre.reshape(TOKENS, KVH, HEAD_SIZE).astype(jnp.bfloat16)
    rows = slot_rows(stored_owner)
    keys_four = stored_keys.reshape(N_FEAT * SLOTS, CTX, KVH, HEAD_SIZE)
    values_four = stored_values.reshape(N_FEAT * SLOTS, CTX, KVH, HEAD_SIZE)
    head_iota = jnp.arange(KVH)
    score_scale = HEAD_SIZE ** (-0.5)
    draft_iota = jnp.arange(DRAFT)
    causal = draft_iota[None, :] <= draft_iota[:, None]

    def request_attention(request):
        start_row = (request * DRAFT).astype(jnp.int32)
        req_query = lax.dynamic_slice_in_dim(query, start_row, DRAFT, 0).reshape(DRAFT, KVH, GROUP, HEAD_SIZE).astype(jnp.float32)
        req_key = lax.dynamic_slice_in_dim(key_new, start_row, DRAFT, 0).astype(jnp.float32)
        req_value = lax.dynamic_slice_in_dim(value_new, start_row, DRAFT, 0).astype(jnp.float32)
        row_here = rows[request]
        old_keys = keys_four[row_here, :, head_iota].astype(jnp.float32)
        old_values = values_four[row_here, :, head_iota].astype(jnp.float32)
        length = stored_lengths[request]
        cache_scores = jnp.einsum('dhgx,hcx->hdgc', req_query, old_keys) * score_scale
        cache_scores = jnp.where(jnp.arange(CTX)[None, None, None, :] < length, cache_scores, -1e+30)
        new_scores = jnp.einsum('dhgx,ehx->hdge', req_query, req_key) * score_scale
        new_scores = jnp.where(causal[None, :, None, :], new_scores, -1e+30)
        row_max = jnp.maximum(lax.optimization_barrier(jnp.max(cache_scores, axis=-1)), lax.optimization_barrier(jnp.max(new_scores, axis=-1)))
        cache_exp = jnp.exp(cache_scores - row_max[..., None])
        new_exp = jnp.exp(new_scores - row_max[..., None])
        total = lax.optimization_barrier(jnp.sum(cache_exp, axis=-1)) + lax.optimization_barrier(jnp.sum(new_exp, axis=-1))
        cache_weights = cache_exp.astype(jnp.bfloat16).astype(jnp.float32)
        new_weights = new_exp.astype(jnp.bfloat16).astype(jnp.float32)
        summed = jnp.einsum('hdgc,hcx->hdgx', cache_weights, old_values) + jnp.einsum('hdge,ehx->hdgx', new_weights, req_value)
        attended = (summed / total[..., None]).astype(jnp.bfloat16)
        return jnp.transpose(attended, (1, 0, 2, 3)).reshape(DRAFT, QUERY_HEADS * HEAD_SIZE)
    attended = lax.map(request_attention, jnp.arange(REQS)).reshape(TOKENS, QUERY_HEADS * HEAD_SIZE)
    return jnp.dot(attended, output_weight, preferred_element_type=jnp.float32).astype(jnp.bfloat16)
```

```python
import functools

import jax
import jax.numpy as jnp
from jax import lax
from jax.experimental import pallas as pl
from jax.experimental.pallas import tpu as pltpu
from jax.sharding import PartitionSpec as P

ADAPTER_RANK = 64
DRAFT = 4
LANES = 128
NEG = -1e30

norm_eps = 1e-05
rope_base = 500000.0


def slot_of(owner_ref, head, requests):
    owners = [owner_ref[r, head] for r in range(requests)]
    slots = []
    for r in range(requests):
        slot = jnp.int32(0)
        for earlier in range(r):
            slot = slot + (owners[earlier] == owners[r]).astype(jnp.int32)
        slots.append(slot)
    return owners, slots


def project_kernel(
    n_feat,
    slot_count,
    requests,
    chunks,
    owner_ref,
    adapter_ref,
    lengths_ref,
    hidden_ref,
    gain_ref,
    wq_hbm,
    wk_hbm,
    wv_hbm,
    wd_hbm,
    *rest,
):
    out_refs = rest[:n_feat]
    rot_ref = rest[n_feat]
    wq, wk, wv, wd, acc, sems = rest[n_feat + 1 :]
    features = hidden_ref.shape[1]
    step = features // chunks
    pairs = ((wq_hbm, wq), (wk_hbm, wk), (wv_hbm, wv), (wd_hbm, wd))
    copies = []
    for c in range(chunks):
        at = pl.ds(c * step, step)
        copies.append(
            [
                pltpu.make_async_copy(src.at[at], dst.at[at], sems.at[c, i])
                for i, (src, dst) in enumerate(pairs)
            ]
        )
        for copy in copies[-1]:
            copy.start()
    me = lax.axis_index("feat")
    head = lax.axis_index("sub")
    tokens = hidden_ref.shape[0]
    rows_dev = slot_count * DRAFT
    rows = n_feat * rows_dev
    query_cols = wq.shape[1]
    head_dim = wk.shape[1]
    owners, slots = slot_of(owner_ref, head, requests)
    row = lax.broadcasted_iota(jnp.int32, (rows, tokens), 0)
    col = lax.broadcasted_iota(jnp.int32, (rows, tokens), 1)
    row1 = lax.broadcasted_iota(jnp.int32, (rows, 1), 0)
    wanted = jnp.full((rows, tokens), -1, jnp.int32)
    adapter = jnp.full((rows, 1), -1, jnp.int32)
    pos_row = lax.broadcasted_iota(jnp.int32, (rows_dev, LANES), 0)
    position = jnp.zeros((rows_dev, LANES), jnp.int32)
    for r in range(requests):
        block = (owners[r] ^ me) * slot_count + slots[r]
        wanted = jnp.where(row // DRAFT == block, r * DRAFT + row % DRAFT, wanted)
        adapter = jnp.where(row1 // DRAFT == block, adapter_ref[r], adapter)
        position = jnp.where(
            pos_row // DRAFT == block, lengths_ref[r] + pos_row % DRAFT, position
        )
    picks = jnp.where(wanted == col, 1.0, 0.0).astype(jnp.bfloat16)
    picked = jnp.dot(picks, hidden_ref[...], preferred_element_type=jnp.float32)
    squares = jnp.sum(picked * picked, axis=1, keepdims=True)
    x = (picked * gain_ref[...].astype(jnp.float32)).astype(jnp.bfloat16)
    lane = lax.broadcasted_iota(jnp.int32, (rows_dev, LANES), 1)
    half = head_dim // 2
    freq = jnp.exp(
        (lane % half).astype(jnp.float32) * (-2.0 / head_dim * jnp.log(jnp.float32(rope_base)))
    )
    angle = position.astype(jnp.float32) * freq
    sine = jnp.sin(angle)
    rot_ref[:, :LANES] = jnp.cos(angle)
    rot_ref[:, LANES:] = jnp.where(lane < half, -sine, sine)
    starts = (0, query_cols, query_cols + head_dim, query_cols + 2 * head_dim)
    for c in range(chunks):
        part = x[:, c * step : (c + 1) * step]
        for i, (_, w) in enumerate(pairs):
            copies[c][i].wait()
            here = slice(starts[i], starts[i] + w.shape[1])
            term = jnp.dot(
                part, w[c * step : (c + 1) * step, :], preferred_element_type=jnp.float32
            )
            if c == 0:
                acc[:, here] = term
            else:
                acc[:, here] += term
    down = acc[:, starts[3] :]
    dcol = lax.broadcasted_iota(jnp.int32, down.shape, 1)
    down = jnp.where(dcol // ADAPTER_RANK == adapter, down, 0.0)
    mid = down[:, :LANES]
    for t in range(1, down.shape[1] // LANES):
        mid = mid + down[:, t * LANES : (t + 1) * LANES]
    squares = jnp.broadcast_to(squares, (rows, LANES))
    for k in range(n_feat):
        at = slice(k * rows_dev, (k + 1) * rows_dev)
        out_refs[k][:, : starts[3]] = acc[at, : starts[3]]
        out_refs[k][:, starts[3] : starts[3] + LANES] = mid[at]
        out_refs[k][:, starts[3] + LANES :] = squares[at]


def attend_kernel(
    n_feat,
    slot_count,
    requests,
    width,
    chunks,
    owner_ref,
    adapter_ref,
    lengths_ref,
    rot_ref,
    *rest,
):
    part_refs = rest[:n_feat]
    up_hbm, keys_hbm, values_hbm, out_ref, up, keys, values, scores, sems, up_sems = rest[n_feat:]
    context, head_dim = keys.shape[1:]
    step = context // chunks
    me = lax.axis_index("feat")
    head = lax.axis_index("sub")
    rows_dev = slot_count * DRAFT
    query_cols = out_ref.shape[1]
    group = query_cols // head_dim
    owners, slots = slot_of(owner_ref, head, requests)
    slot_adapter = [jnp.int32(0)] * slot_count
    slot_length = [jnp.int32(0)] * slot_count
    for r in range(requests):
        for s in range(slot_count):
            mine = jnp.logical_and(owners[r] == me, slots[r] == s)
            slot_adapter[s] = jnp.where(mine, adapter_ref[r], slot_adapter[s])
            slot_length[s] = jnp.where(mine, lengths_ref[r], slot_length[s])
    per = LANES // ADAPTER_RANK
    up_copies = []
    for s in range(slot_count):
        start = pl.multiple_of(slot_adapter[s] // per * LANES, LANES)
        up_copies.append(
            pltpu.make_async_copy(up_hbm.at[pl.ds(start, LANES)], up.at[s], up_sems.at[s])
        )
        up_copies[-1].start()
    copies = []
    for i, (src, dst) in enumerate(((keys_hbm, keys), (values_hbm, values))):
        for c in range(chunks):
            at = pl.ds(c * step, step)
            copy = pltpu.make_async_copy(src.at[:, at], dst.at[:, at], sems.at[i, c])
            copy.start()
            copies.append(copy)
    total = part_refs[0][...]
    for ref in part_refs[1:]:
        total = total + ref[...]
    base = query_cols + 2 * head_dim
    scale = lax.rsqrt(total[:, base + LANES :] / width + norm_eps)
    row = lax.broadcasted_iota(jnp.int32, (rows_dev, 1), 0)
    mid = total[:, base : base + LANES] * scale
    mid_hi = mid.astype(jnp.bfloat16)
    rest1 = mid - mid_hi.astype(jnp.float32)
    mid_lo = rest1.astype(jnp.bfloat16)
    both = jnp.concatenate([mid_hi, mid_lo], axis=0)
    delta = jnp.zeros((rows_dev, query_cols), jnp.float32)
    for s in range(slot_count):
        up_copies[s].wait()
        d = jnp.dot(both, up[s], preferred_element_type=jnp.float32)
        delta = jnp.where(row // DRAFT == s, d[:rows_dev] + d[rows_dev:], delta)
    cosine = rot_ref[:, :LANES]
    sine = rot_ref[:, LANES:]
    half = head_dim // 2

    def rotate(v):
        return v * cosine + pltpu.roll(v, half, 1) * sine

    plain = []
    wide = []
    for g in range(group):
        at = slice(g * head_dim, (g + 1) * head_dim)
        q = rotate(total[:, at] * scale + delta[:, at])
        plain.append(q)
        wide.append(
            jnp.concatenate(
                [jnp.where(row // DRAFT == s, q, 0.0) for s in range(slot_count)], axis=1
            )
        )
    plain = jnp.concatenate(plain, axis=0).astype(jnp.bfloat16)
    wide = jnp.concatenate(wide, axis=0).astype(jnp.bfloat16)
    key_new = rotate(total[:, query_cols : query_cols + head_dim] * scale).astype(jnp.bfloat16)
    value_new = (total[:, query_cols + head_dim : base] * scale).astype(jnp.bfloat16)
    q_rows = group * rows_dev
    nt = (((1,), (1,)), ((), ()))
    score_scale = head_dim ** (-0.5)
    new = lax.dot_general(plain, key_new, nt, preferred_element_type=jnp.float32) * score_scale
    nrow = lax.broadcasted_iota(jnp.int32, new.shape, 0) % rows_dev
    ncol = lax.broadcasted_iota(jnp.int32, new.shape, 1)
    seen = jnp.logical_and(nrow // DRAFT == ncol // DRAFT, ncol <= nrow)
    new = jnp.where(seen, new, NEG)
    qrow = lax.broadcasted_iota(jnp.int32, (q_rows, 1), 0) % rows_dev
    length = jnp.zeros((q_rows, 1), jnp.int32)
    for s in range(slot_count):
        length = jnp.where(qrow // DRAFT == s, slot_length[s], length)
    peak = jnp.full((q_rows, LANES), NEG, jnp.float32)
    for c in range(chunks):
        copies[c].wait()
        at = slice(c * step, (c + 1) * step)
        kc = jnp.concatenate([keys[s, at] for s in range(slot_count)], axis=1)
        sc = lax.dot_general(wide, kc, nt, preferred_element_type=jnp.float32) * score_scale
        col = lax.broadcasted_iota(jnp.int32, sc.shape, 1) + c * step
        sc = jnp.where(col < length, sc, NEG)
        scores[:, at] = sc
        for t in range(step // LANES):
            peak = jnp.maximum(peak, sc[:, t * LANES : (t + 1) * LANES])
    top = jnp.maximum(jnp.max(peak, axis=1, keepdims=True), jnp.max(new, axis=1, keepdims=True))
    new_e = jnp.exp(new - top)
    acc_sum = jnp.zeros((q_rows, LANES), jnp.float32)
    acc = jnp.zeros((q_rows, slot_count * head_dim), jnp.float32)
    for c in range(chunks):
        copies[chunks + c].wait()
        at = slice(c * step, (c + 1) * step)
        e = jnp.exp(scores[:, at] - top)
        for t in range(step // LANES):
            acc_sum = acc_sum + e[:, t * LANES : (t + 1) * LANES]
        vc = jnp.concatenate([values[s, at] for s in range(slot_count)], axis=1)
        acc = acc + jnp.dot(e.astype(jnp.bfloat16), vc, preferred_element_type=jnp.float32)
    summed = jnp.zeros((q_rows, head_dim), jnp.float32)
    for s in range(slot_count):
        summed = jnp.where(
            qrow // DRAFT == s, acc[:, s * head_dim : (s + 1) * head_dim], summed
        )
    summed = summed + jnp.dot(
        new_e.astype(jnp.bfloat16), value_new, preferred_element_type=jnp.float32
    )
    denom = jnp.sum(acc_sum, axis=1, keepdims=True) + jnp.sum(new_e, axis=1, keepdims=True)
    attended = summed / denom
    for g in range(group):
        out_ref[:, g * head_dim : (g + 1) * head_dim] = attended[
            g * rows_dev : (g + 1) * rows_dev
        ].astype(jnp.bfloat16)


def output_kernel(n_feat, n_sub, slot_count, requests, chunks, owner_ref, *rest):
    att_refs = rest[:n_feat]
    w_hbm = rest[n_feat]
    out_refs = rest[n_feat + 1 : n_feat + 1 + n_sub]
    w, sems = rest[n_feat + 1 + n_sub :]
    step = w.shape[1] // chunks
    copies = []
    for c in range(chunks):
        at = pl.ds(c * step, step)
        copies.append(pltpu.make_async_copy(w_hbm.at[:, at], w.at[:, at], sems.at[c]))
        copies[-1].start()
    me = lax.axis_index("feat")
    head = lax.axis_index("sub")
    rows_dev = slot_count * DRAFT
    rows = n_feat * rows_dev
    rows_out = out_refs[0].shape[0]
    tokens = n_sub * rows_out
    owners, slots = slot_of(owner_ref, head, requests)
    row = lax.broadcasted_iota(jnp.int32, (tokens, rows), 0)
    col = lax.broadcasted_iota(jnp.int32, (tokens, rows), 1)
    token = (row // rows_out ^ head) * rows_out + row % rows_out
    wanted = jnp.full((tokens, rows), -1, jnp.int32)
    for r in range(requests):
        start = ((owners[r] ^ me) * slot_count + slots[r]) * DRAFT
        wanted = jnp.where(token // DRAFT == r, start + token % DRAFT, wanted)
    picks = jnp.where(wanted == col, 1.0, 0.0).astype(jnp.bfloat16)
    held = jnp.concatenate([ref[...].astype(jnp.float32) for ref in att_refs], axis=0)
    x = jnp.dot(picks, held.astype(jnp.bfloat16), preferred_element_type=jnp.float32).astype(
        jnp.bfloat16
    )
    for c in range(chunks):
        copies[c].wait()
        at = slice(c * step, (c + 1) * step)
        y = jnp.dot(x, w[:, at], preferred_element_type=jnp.float32)
        for k in range(n_sub):
            out_refs[k][:, at] = y[k * rows_out : (k + 1) * rows_out].astype(jnp.bfloat16)


SMEM = pl.BlockSpec(memory_space=pltpu.SMEM)
VMEM = pl.BlockSpec(memory_space=pltpu.VMEM)
ANY = pl.BlockSpec(memory_space=pl.ANY)
MIB = 1 << 20


def body(
    hidden,
    input_norm_gain,
    query_weight,
    key_weight,
    value_weight,
    adapter_down_weight,
    adapter_up_weight,
    output_weight,
    request_adapter,
    stored_owner,
    stored_lengths,
    stored_keys,
    stored_values,
):
    n_feat = lax.axis_size("feat")
    n_sub = lax.axis_size("sub")
    tokens, features = hidden.shape
    query_cols = query_weight.shape[1]
    head_dim = key_weight.shape[1]
    slot_count, context, _ = stored_keys.shape
    requests = request_adapter.shape[0]
    rows_dev = slot_count * DRAFT
    down_cols = adapter_down_weight.shape[1]
    out_cols = output_weight.shape[1]
    block_cols = query_cols + 2 * head_dim + 2 * LANES
    bf16 = jnp.bfloat16
    f32 = jnp.float32

    chunks = 4
    *parts, rot = pl.pallas_call(
        functools.partial(project_kernel, n_feat, slot_count, requests, chunks),
        out_shape=[jax.ShapeDtypeStruct((rows_dev, block_cols), f32)] * n_feat
        + [jax.ShapeDtypeStruct((rows_dev, 2 * LANES), f32)],
        in_specs=[SMEM] * 3 + [VMEM] * 2 + [ANY] * 4,
        out_specs=[VMEM] * (n_feat + 1),
        scratch_shapes=[
            pltpu.VMEM((features, query_cols), bf16),
            pltpu.VMEM((features, head_dim), bf16),
            pltpu.VMEM((features, head_dim), bf16),
            pltpu.VMEM((features, down_cols), bf16),
            pltpu.VMEM((n_feat * rows_dev, query_cols + 2 * head_dim + down_cols), f32),
            pltpu.SemaphoreType.DMA((chunks, 4)),
        ],
        compiler_params=pltpu.CompilerParams(vmem_limit_bytes=24 * MIB),
        name="project",
    )(
        stored_owner,
        request_adapter,
        stored_lengths,
        hidden,
        input_norm_gain.reshape(1, features),
        query_weight,
        key_weight,
        value_weight,
        adapter_down_weight,
    )

    def spread(blocks, axis, size):
        got = [blocks[0]]
        for k in range(1, size):
            got.append(lax.ppermute(blocks[k], axis, [(i, i ^ k) for i in range(size)]))
        return got

    parts = spread(parts, "feat", n_feat)
    chunks = 8
    attended = pl.pallas_call(
        functools.partial(
            attend_kernel, n_feat, slot_count, requests, n_feat * features, chunks
        ),
        out_shape=jax.ShapeDtypeStruct((rows_dev, query_cols), bf16),
        in_specs=[SMEM] * 3 + [VMEM] * (n_feat + 1) + [ANY] * 3,
        out_specs=VMEM,
        scratch_shapes=[
            pltpu.VMEM((slot_count, LANES, query_cols), bf16),
            pltpu.VMEM(stored_keys.shape, bf16),
            pltpu.VMEM(stored_values.shape, bf16),
            pltpu.VMEM((rows_dev * query_cols // head_dim, context), f32),
            pltpu.SemaphoreType.DMA((2, chunks)),
            pltpu.SemaphoreType.DMA((slot_count,)),
        ],
        compiler_params=pltpu.CompilerParams(vmem_limit_bytes=24 * MIB),
        name="attend",
    )(
        stored_owner,
        request_adapter,
        stored_lengths,
        rot,
        *parts,
        adapter_up_weight,
        stored_keys,
        stored_values,
    )
    held = spread([attended] * n_feat, "feat", n_feat)
    chunks = 4
    outs = pl.pallas_call(
        functools.partial(output_kernel, n_feat, n_sub, slot_count, requests, chunks),
        out_shape=[jax.ShapeDtypeStruct((tokens // n_sub, out_cols), bf16)] * n_sub,
        in_specs=[SMEM] + [VMEM] * n_feat + [ANY],
        out_specs=[VMEM] * n_sub,
        scratch_shapes=[
            pltpu.VMEM(output_weight.shape, bf16),
            pltpu.SemaphoreType.DMA((chunks,)),
        ],
        compiler_params=pltpu.CompilerParams(vmem_limit_bytes=16 * MIB),
        name="output",
    )(stored_owner, *held, output_weight)
    outs = spread(outs, "sub", n_sub)
    total = outs[0].astype(f32)
    for part in outs[1:]:
        total = total + part.astype(f32)
    return total.astype(bf16)


def solution(mesh):
    in_specs = (
        P("groups", "feat"),
        P("feat"),
        P("feat", "sub"),
        P("feat", "sub"),
        P("feat", "sub"),
        P("feat", None),
        P(None, "sub"),
        P("sub", "feat"),
        P("groups"),
        P("groups", None),
        P("groups"),
        P(("groups", "feat"), None, "sub"),
        P(("groups", "feat"), None, "sub"),
    )
    out_specs = P(("groups", "sub"), "feat")
    return jax.shard_map(body, mesh=mesh, in_specs=in_specs, out_specs=out_specs, check_vma=False)
```

```python
import functools

import jax
import jax.numpy as jnp
from jax import lax
from jax.experimental import pallas as pl
from jax.experimental.pallas import tpu as pltpu
from jax.sharding import PartitionSpec as P


ADAPTER_RANK = 64
DRAFT = 4
LANES = 128
NEG = -1e30
LOG2E = 1.4426950408889634

norm_eps = 1e-05
rope_base = 500000.0


def step_to(name, source, target, size):
    if CYCLIC[name]:
        return lax.rem(target - source + size, size)
    return source ^ target


def slot_of(owner_ref, head, requests):
    owners = [owner_ref[r, head] for r in range(requests)]
    slots = []
    for r in range(requests):
        slot = jnp.int32(0)
        for earlier in range(r):
            slot = slot + (owners[earlier] == owners[r]).astype(jnp.int32)
        slots.append(slot)
    return owners, slots


def project_kernel(
    n_feat,
    n_sub,
    slot_count,
    requests,
    chunks,
    owner_hbm,
    adapter_hbm,
    lengths_hbm,
    hidden_hbm,
    gain_hbm,
    wq_hbm,
    wk_hbm,
    wv_hbm,
    wd_hbm,
    up_hbm,
    *rest,
):
    out_refs = rest[:n_feat]
    rot_ref, length_ref, picks_ref, up_ref = rest[n_feat : n_feat + 4]
    owner_ref, adapter_ref, lengths_ref, hidden_ref, gain_ref = rest[n_feat + 4 : n_feat + 9]
    wq, wk, wv, wd, acc, sums_ref, sems, small_sems, up_sems = rest[n_feat + 9 :]
    inputs = [
        pltpu.make_async_copy(hidden_hbm, hidden_ref, small_sems.at[0]),
        pltpu.make_async_copy(gain_hbm, gain_ref, small_sems.at[1]),
    ]
    scalars = [
        pltpu.make_async_copy(src, dst, small_sems.at[2 + i])
        for i, (src, dst) in enumerate(
            ((owner_hbm, owner_ref), (adapter_hbm, adapter_ref), (lengths_hbm, lengths_ref))
        )
    ]
    features = hidden_ref.shape[1]
    step = features // chunks
    cuts = [slice(c * step, (c + 1) * step) for c in range(chunks)]
    whole = slice(0, features)
    pieces = [(wq_hbm, wq, 0, cut) for cut in cuts]
    pieces.insert(1, (wd_hbm, wd, 1, whole))
    pieces += [(wk_hbm, wk, 2, whole), (wv_hbm, wv, 3, whole)]
    copies = [
        pltpu.make_async_copy(
            src.at[pl.ds(cut.start, cut.stop - cut.start)],
            dst.at[pl.ds(cut.start, cut.stop - cut.start)],
            sems.at[i],
        )
        for i, (src, dst, _, cut) in enumerate(pieces)
    ]
    for copy in copies[:1] + inputs + copies[1:2] + scalars + copies[2:]:
        copy.start()
    me = lax.axis_index("feat")
    head = lax.axis_index("sub")
    tokens = hidden_ref.shape[0]
    rows_dev = slot_count * DRAFT
    rows = n_feat * rows_dev
    query_cols = wq.shape[1]
    head_dim = wk.shape[1]
    for copy in inputs:
        copy.wait()
    h = hidden_ref[...].astype(jnp.float32)
    squares = jnp.sum(h * h, axis=1, keepdims=True)
    x = (h * gain_ref[...].astype(jnp.float32)[None, :]).astype(jnp.bfloat16)
    for copy in scalars:
        copy.wait()
    owners, slots = slot_of(owner_ref, head, requests)
    blocks = [
        step_to("sums", me, owners[r], n_feat) * slot_count + slots[r] for r in range(requests)
    ]
    sources = [
        step_to("held", owners[r], me, n_feat) * slot_count + slots[r] for r in range(requests)
    ]
    per = LANES // ADAPTER_RANK
    up_copies = []
    for s in range(slot_count):
        mine = jnp.int32(0)
        for r in range(requests):
            mine = jnp.where(blocks[r] == s, adapter_ref[r], mine)
        start = pl.multiple_of(mine // per * LANES, LANES)
        up_copies.append(
            pltpu.make_async_copy(up_hbm.at[pl.ds(start, LANES)], up_ref.at[s], up_sems.at[s])
        )
        up_copies[-1].start()
    row = lax.broadcasted_iota(jnp.int32, (rows, tokens), 0)
    col = lax.broadcasted_iota(jnp.int32, (rows, tokens), 1)
    wanted = jnp.full((rows, tokens), -1, jnp.int32)
    token1 = lax.broadcasted_iota(jnp.int32, (tokens, 1), 0)
    adapter = jnp.full((tokens, 1), -1, jnp.int32)
    dev_row = lax.broadcasted_iota(jnp.int32, (rows_dev, LANES), 0)
    length = jnp.zeros((rows_dev, LANES), jnp.int32)
    out_row = lax.broadcasted_iota(jnp.int32, (tokens, rows), 0)
    out_col = lax.broadcasted_iota(jnp.int32, (tokens, rows), 1)
    rows_out = tokens // n_sub
    out_block = out_row // rows_out
    if CYCLIC["outs"]:
        out_block = lax.rem(out_block + head, n_sub)
    else:
        out_block = out_block ^ head
    token = out_block * rows_out + out_row % rows_out
    source = jnp.full((tokens, rows), -1, jnp.int32)
    for r in range(requests):
        block = blocks[r]
        wanted = jnp.where(row // DRAFT == block, r * DRAFT + row % DRAFT, wanted)
        adapter = jnp.where(token1 // DRAFT == r, adapter_ref[r], adapter)
        length = jnp.where(dev_row // DRAFT == block, lengths_ref[r], length)
        source = jnp.where(token // DRAFT == r, sources[r] * DRAFT + token % DRAFT, source)
    picks_ref[...] = jnp.where(source == out_col, 1.0, 0.0).astype(jnp.bfloat16)
    length_ref[...] = length
    route = jnp.where(wanted == col, 1.0, 0.0).astype(jnp.bfloat16)
    lane = lax.broadcasted_iota(jnp.int32, (rows_dev, LANES), 1)
    half = head_dim // 2
    freq = jnp.exp(
        (lane % half).astype(jnp.float32) * (-2.0 / head_dim * jnp.log(jnp.float32(rope_base)))
    )
    angle = (length + dev_row % DRAFT).astype(jnp.float32) * freq
    sine = jnp.sin(angle)
    rot_ref[:, :LANES] = jnp.cos(angle)
    rot_ref[:, LANES:] = jnp.where(lane < half, -sine, sine)
    bf16 = jnp.bfloat16
    squares_hi = squares.astype(bf16).astype(jnp.float32)
    squares = jnp.where(
        lax.broadcasted_iota(jnp.int32, (tokens, LANES), 1) < LANES // 2,
        squares_hi,
        squares - squares_hi,
    )
    starts = (0, query_cols, query_cols + wd.shape[1], query_cols + wd.shape[1] + head_dim)
    begun = set()
    for copy, (_, w, i, cut) in zip(copies, pieces):
        copy.wait()
        here = slice(starts[i], starts[i] + w.shape[1])
        term = jnp.dot(x[:, cut], w[cut, :], preferred_element_type=jnp.float32)
        if i in begun:
            acc[:, here] += term
        else:
            acc[:, here] = term
        begun.add(i)
    down = acc[:, starts[1] : starts[2]]
    dcol = lax.broadcasted_iota(jnp.int32, down.shape, 1)
    down = jnp.where(dcol // ADAPTER_RANK == adapter, down, 0.0)
    mid = down[:, :LANES]
    for t in range(1, down.shape[1] // LANES):
        mid = mid + down[:, t * LANES : (t + 1) * LANES]
    base = query_cols + 2 * head_dim
    sums_ref[:, :query_cols] = acc[:, :query_cols].astype(bf16)
    sums_ref[:, query_cols:base] = acc[:, starts[2] :].astype(bf16)
    sums_ref[:, base : base + LANES] = mid.astype(bf16)
    sums_ref[:, base + LANES :] = squares.astype(bf16)
    routed = jnp.dot(route, sums_ref[...], preferred_element_type=jnp.float32)
    for k, ref in enumerate(out_refs):
        ref[...] = routed[k * rows_dev : (k + 1) * rows_dev].astype(bf16)
    for copy in up_copies:
        copy.wait()


def turn_kernel(chunks, keys, values, after_ref, out_ref):
    del values, after_ref
    slot_count, context, head_dim = keys.shape
    step = context // chunks
    for c in range(chunks):
        at = slice(c * step, (c + 1) * step)
        for s in range(slot_count):
            out_ref[s * head_dim : (s + 1) * head_dim, at] = keys[s, at].T


def at_multiple(start, size):
    if not isinstance(start, int):
        start = pl.multiple_of(start, size)
    return pl.ds(start, size)


def attend_kernel(
    n_parts,
    width,
    blocks,
    chunks,
    rot_ref,
    length_ref,
    up,
    keys,
    values,
    *rest,
):
    part_refs = rest[:n_parts]
    out_ref, scores = rest[n_parts:]
    slot_count, context, head_dim = values.shape
    rows_dev = slot_count * DRAFT
    query_cols = out_ref.shape[1]
    group = query_cols // head_dim
    total = part_refs[0][...].astype(jnp.float32)
    for ref in part_refs[1:]:
        total = total + ref[...].astype(jnp.float32)
    base = query_cols + 2 * head_dim
    squares = total[:, base + LANES :]
    squares = squares + pltpu.roll(squares, LANES // 2, 1)
    scale = lax.rsqrt(squares / width + norm_eps)
    row = lax.broadcasted_iota(jnp.int32, (rows_dev, 1), 0)
    mid = total[:, base : base + LANES]
    mid_hi = mid.astype(jnp.bfloat16)
    mid_lo = (mid - mid_hi.astype(jnp.float32)).astype(jnp.bfloat16)
    both = jnp.concatenate([mid_hi, mid_lo], axis=0)
    delta = jnp.zeros((rows_dev, query_cols), jnp.float32)
    for s in range(slot_count):
        d = jnp.dot(both, up[s], preferred_element_type=jnp.float32)
        delta = jnp.where(row // DRAFT == s, d[:rows_dev] + d[rows_dev:], delta)
    cosine = rot_ref[:, :LANES]
    sine = rot_ref[:, LANES:]
    half = head_dim // 2

    def rotate(v):
        return v * cosine + pltpu.roll(v, half, 1) * sine

    plain = []
    wide = []
    for g in range(group):
        at = slice(g * head_dim, (g + 1) * head_dim)
        q = rotate((total[:, at] + delta[:, at]) * scale)
        plain.append(q)
        wide.append(
            jnp.concatenate(
                [jnp.where(row // DRAFT == s, q, 0.0) for s in range(slot_count)], axis=1
            )
        )
    plain = jnp.concatenate(plain, axis=0).astype(jnp.bfloat16)
    wide = jnp.concatenate(wide, axis=0).astype(jnp.bfloat16)
    key_new = rotate(total[:, query_cols : query_cols + head_dim] * scale).astype(jnp.bfloat16)
    value_new = (total[:, query_cols + head_dim : base] * scale).astype(jnp.bfloat16)
    q_rows = group * rows_dev
    nt = (((1,), (1,)), ((), ()))
    to_exponent = head_dim ** (-0.5) * LOG2E
    new = lax.dot_general(plain, key_new, nt, preferred_element_type=jnp.float32)
    nrow = lax.broadcasted_iota(jnp.int32, new.shape, 0) % rows_dev
    ncol = lax.broadcasted_iota(jnp.int32, new.shape, 1)
    seen = jnp.logical_and(nrow // DRAFT == ncol // DRAFT, ncol <= nrow)
    new = jnp.where(seen, new, NEG)
    qrow = lax.broadcasted_iota(jnp.int32, (q_rows, 1), 0) % rows_dev
    left = length_ref[...] - lax.broadcasted_iota(jnp.int32, (rows_dev, LANES), 1)
    block = context // blocks
    step = block // chunks

    def score(first, c, peak):
        kc = keys[:, at_multiple(first + c * step, step)]
        sc = jnp.dot(wide, kc, preferred_element_type=jnp.float32)
        for t in range(step // LANES):
            start = first + c * step + t * LANES
            tile = sc[:, t * LANES : (t + 1) * LANES].reshape(group, rows_dev, LANES)
            tile = jnp.where((left > start)[None], tile, NEG).reshape(q_rows, LANES)
            scores[:, at_multiple(start, LANES)] = tile
            peak = jnp.maximum(peak, tile)
        return peak

    def weigh(first, c, top, acc, acc_sum):
        es = []
        for t in range(step // LANES):
            start = first + c * step + t * LANES
            raw = scores[:, at_multiple(start, LANES)]
            e = jnp.exp2((raw - top) * to_exponent)
            acc_sum = acc_sum + e
            es.append(e.astype(jnp.bfloat16))
        at = at_multiple(first + c * step, step)
        vc = jnp.concatenate([values[s, at] for s in range(slot_count)], axis=1)
        acc = acc + jnp.dot(jnp.concatenate(es, axis=1), vc, preferred_element_type=jnp.float32)
        return acc, acc_sum

    def raise_top(peak, top, acc, acc_sum):
        higher = jnp.maximum(top, jnp.max(peak, axis=1, keepdims=True))
        fade = jnp.exp2((top - higher) * to_exponent)
        acc = acc * jnp.concatenate([fade] * (acc.shape[1] // LANES), axis=1)
        return higher, acc, acc_sum * fade

    def advance(n, carry):
        peak, top, acc, acc_sum = carry
        top, acc, acc_sum = raise_top(peak, top, acc, acc_sum)
        peak = jnp.full((q_rows, LANES), NEG, jnp.float32)
        for c in range(chunks):
            peak = score(n * block, c, peak)
            acc, acc_sum = weigh((n - 1) * block, c, top, acc, acc_sum)
        return peak, top, acc, acc_sum

    peak = jnp.full((q_rows, LANES), NEG, jnp.float32)
    for c in range(chunks):
        peak = score(0, c, peak)
    top = jnp.broadcast_to(jnp.max(new, axis=1, keepdims=True), (q_rows, LANES))
    acc = jnp.zeros((q_rows, slot_count * head_dim), jnp.float32)
    acc_sum = jnp.zeros((q_rows, LANES), jnp.float32)
    for n in range(1, blocks):
        peak, top, acc, acc_sum = advance(n, (peak, top, acc, acc_sum))
    top, acc, acc_sum = raise_top(peak, top, acc, acc_sum)
    for c in range(chunks):
        acc, acc_sum = weigh((blocks - 1) * block, c, top, acc, acc_sum)
    new_e = jnp.exp2((new - top[:, : new.shape[1]]) * to_exponent)
    summed = jnp.zeros((q_rows, head_dim), jnp.float32)
    for s in range(slot_count):
        summed = jnp.where(
            qrow // DRAFT == s, acc[:, s * head_dim : (s + 1) * head_dim], summed
        )
    summed = summed + jnp.dot(
        new_e.astype(jnp.bfloat16), value_new, preferred_element_type=jnp.float32
    )
    denom = jnp.sum(acc_sum, axis=1, keepdims=True) + jnp.sum(new_e, axis=1, keepdims=True)
    attended = summed / denom
    for g in range(group):
        out_ref[:, g * head_dim : (g + 1) * head_dim] = attended[
            g * rows_dev : (g + 1) * rows_dev
        ].astype(jnp.bfloat16)


def output_kernel(n_feat, chunks, picks_ref, w, *rest):
    held_refs = rest[:n_feat]
    out_refs = rest[n_feat:]
    step = w.shape[1] // chunks
    rows_out = out_refs[0].shape[0]
    f32 = jnp.float32
    held = jnp.concatenate([ref[...].astype(f32) for ref in held_refs], axis=0)
    x = jnp.dot(picks_ref[...], held.astype(jnp.bfloat16), preferred_element_type=f32)
    x = x.astype(jnp.bfloat16)
    for c in range(chunks):
        at = slice(c * step, (c + 1) * step)
        y = jnp.dot(x, w[:, at], preferred_element_type=f32)
        for k, ref in enumerate(out_refs):
            ref[:, at] = y[k * rows_out : (k + 1) * rows_out].astype(jnp.bfloat16)


VMEM = pl.BlockSpec(memory_space=pltpu.VMEM)
HBM = pl.BlockSpec(memory_space=pltpu.HBM)
MIB = 1 << 20
CYCLIC = {"sums": False, "held": True, "outs": True}
ATT_MIB = 8
ATT_BLOCKS = 4
ATT_CHUNKS = 4
ATT_COST = 2
FETCH_COST = 4
PROJ_MIB = 10
PROJ_COST = 2


def body(
    hidden,
    input_norm_gain,
    query_weight,
    key_weight,
    value_weight,
    adapter_down_weight,
    adapter_up_weight,
    output_weight,
    request_adapter,
    stored_owner,
    stored_lengths,
    stored_keys,
    stored_values,
):
    n_feat = lax.axis_size("feat")
    n_sub = lax.axis_size("sub")
    tokens, features = hidden.shape
    query_cols = query_weight.shape[1]
    head_dim = key_weight.shape[1]
    slot_count, context, _ = stored_keys.shape
    requests = request_adapter.shape[0]
    rows_dev = slot_count * DRAFT
    down_cols = adapter_down_weight.shape[1]
    out_cols = output_weight.shape[1]
    block_cols = query_cols + 2 * head_dim + 2 * LANES
    bf16 = jnp.bfloat16
    f32 = jnp.float32

    def stay(array):
        return pltpu.with_memory_space_constraint(array, pltpu.HBM)

    chunks = 2
    rows = n_feat * rows_dev
    *parts, rot, length, picks, up = pl.pallas_call(
        functools.partial(project_kernel, n_feat, n_sub, slot_count, requests, chunks),
        out_shape=[jax.ShapeDtypeStruct((rows_dev, block_cols), bf16)] * n_feat
        + [
            jax.ShapeDtypeStruct((rows_dev, 2 * LANES), f32),
            jax.ShapeDtypeStruct((rows_dev, LANES), jnp.int32),
            jax.ShapeDtypeStruct((tokens, rows), bf16),
            jax.ShapeDtypeStruct((slot_count, LANES, query_cols), bf16),
        ],
        in_specs=[HBM] * 10,
        out_specs=[VMEM] * (n_feat + 4),
        scratch_shapes=[
            pltpu.SMEM(stored_owner.shape, jnp.int32),
            pltpu.SMEM(request_adapter.shape, jnp.int32),
            pltpu.SMEM(stored_lengths.shape, jnp.int32),
            pltpu.VMEM(hidden.shape, bf16),
            pltpu.VMEM(input_norm_gain.shape, bf16),
            pltpu.VMEM((features, query_cols), bf16),
            pltpu.VMEM((features, head_dim), bf16),
            pltpu.VMEM((features, head_dim), bf16),
            pltpu.VMEM((features, down_cols), bf16),
            pltpu.VMEM((tokens, query_cols + 2 * head_dim + down_cols), f32),
            pltpu.VMEM((tokens, block_cols), bf16),
            pltpu.SemaphoreType.DMA((chunks + 3,)),
            pltpu.SemaphoreType.DMA((5,)),
            pltpu.SemaphoreType.DMA((slot_count,)),
        ],
        compiler_params=pltpu.CompilerParams(vmem_limit_bytes=PROJ_MIB * MIB),
        cost_estimate=pl.CostEstimate(
            flops=0, bytes_accessed=PROJ_COST * query_weight.size * 2, transcendentals=0
        ),
        name="project",
    )(
        *map(
            stay,
            (
                stored_owner,
                request_adapter,
                stored_lengths,
                hidden,
                input_norm_gain,
                query_weight,
                key_weight,
                value_weight,
                adapter_down_weight,
                adapter_up_weight,
            ),
        )
    )

    def spread(blocks, axis, size, name):
        got = [blocks[0]]
        for j in range(1, size):
            pairs = [(i, (i + j) % size if CYCLIC[name] else i ^ j) for i in range(size)]
            got.append(lax.ppermute(blocks[j], axis, pairs))
        return got

    parts = spread(parts, "feat", n_feat, "sums")
    keys = pl.pallas_call(
        functools.partial(turn_kernel, 16),
        out_shape=jax.ShapeDtypeStruct((slot_count * head_dim, context), bf16),
        in_specs=[VMEM] * 3,
        out_specs=VMEM,
        compiler_params=pltpu.CompilerParams(vmem_limit_bytes=4 * MIB),
        cost_estimate=pl.CostEstimate(
            flops=0, bytes_accessed=FETCH_COST * stored_keys.size * 2, transcendentals=0
        ),
        name="turn",
    )(stored_keys, stored_values, rot)
    attended = pl.pallas_call(
        functools.partial(attend_kernel, len(parts), n_feat * features, ATT_BLOCKS, ATT_CHUNKS),
        out_shape=jax.ShapeDtypeStruct((rows_dev, query_cols), bf16),
        in_specs=[VMEM] * (len(parts) + 5),
        out_specs=VMEM,
        scratch_shapes=[pltpu.VMEM((rows_dev * query_cols // head_dim, context), f32)],
        compiler_params=pltpu.CompilerParams(vmem_limit_bytes=ATT_MIB * MIB),
        cost_estimate=pl.CostEstimate(
            flops=0, bytes_accessed=ATT_COST * stored_keys.size * 2, transcendentals=0
        ),
        name="attend",
    )(rot, length, up, keys, stored_values, *parts)
    held = spread([attended] * n_feat, "feat", n_feat, "held")
    outs = pl.pallas_call(
        functools.partial(output_kernel, n_feat, 4),
        out_shape=[jax.ShapeDtypeStruct((tokens // n_sub, out_cols), bf16)] * n_sub,
        in_specs=[VMEM] * (len(held) + 2),
        out_specs=[VMEM] * n_sub,
        compiler_params=pltpu.CompilerParams(vmem_limit_bytes=16 * MIB),
        name="output",
    )(picks, output_weight, *held)
    outs = spread(outs, "sub", n_sub, "outs")
    total = outs[0].astype(f32)
    for part in outs[1:]:
        total = total + part.astype(f32)
    return total.astype(bf16)


def solution(mesh):
    in_specs = (
        P("groups", "feat"),
        P("feat"),
        P("feat", "sub"),
        P("feat", "sub"),
        P("feat", "sub"),
        P("feat", None),
        P(None, "sub"),
        P("sub", "feat"),
        P("groups"),
        P("groups", None),
        P("groups"),
        P(("groups", "feat"), None, "sub"),
        P(("groups", "feat"), None, "sub"),
    )
    out_specs = P(("groups", "sub"), "feat")


    return jax.shard_map(body, mesh=mesh, in_specs=in_specs, out_specs=out_specs, check_vma=False)
```
